32 devices in a mesh: seq: 16 (over z, x, core), head: 2 (over y).
Axes of the slice: x: 2, y: 2, z: 4, core: 2. Of those that a mesh axis runs over, the one named last changes fastest.
Arguments:
- queries: bfloat16 [2, 1024, 4096], P(None, ('seq', 'head')), may hold values from -6 to 6
- keys: bfloat16 [2, 1024, 4096], P(None, ('seq', 'head')), may hold values from -6 to 6
- values: bfloat16 [2, 1024, 4096], P(None, ('seq', 'head')), may hold values from -6 to 6
- rates: bfloat16 [2, 1024, 8], P(None, ('seq', 'head')), may hold values from 0.049804688 to 1
- fast_init: float32 [8, 3, 512, 256], P('head', None, 'seq'), may hold values from -0.25 to 0.25
Outputs:
- outputs: bfloat16 [2, 1024, 4096], P(None, 'seq', 'head')
The draws below stay inside these ranges and needn't reach their ends.
All inputs are finite; a program needn't handle non-finite values.
Results may differ from the reference program's by a relative error of at most 0.0085.
Values may be sent and summed in bfloat16 or wider, within the bound.
No kernel may reach another device: no remote copies, remote signals or barrier semaphores. Data moves between devices by JAX's collectives and lax.ppermute only.
A program may use at most 64 MiB of HBM per device.

```python
import math
import jax
import jax.numpy as jnp
from jax import lax

HEADS = 8
HD = 512
FH = 256
BLOCK_COUNT = 2
BLOCK_TOKENS = 1024
D = 4096


def shard_levels(key, dims, split, least, largest):
    level = 1.0
    for axis_at, blocks in split:
        draws = jax.random.uniform(jax.random.fold_in(jax.random.fold_in(key, 6), axis_at), (blocks,), jnp.float32, least / len(split), largest / len(split))
        level = level * jnp.repeat(jnp.exp(draws), dims[axis_at] // blocks).reshape((-1,) + (1,) * (len(dims) - 1 - axis_at))
    return level


def noise(key, shape, deviation, most, pieces=(), kind=jnp.bfloat16):
    values = deviation * jax.random.normal(key, shape, jnp.float32)
    if pieces:
        values = values * shard_levels(key, shape, pieces, -0.22, 0.18)
    return jnp.clip(values, -most, most).astype(kind)


def setup_inputs(seed: int = 0) -> dict:
    key_list = jax.random.split(jax.random.key(seed), 6)
    queries = noise(key_list[0], (BLOCK_COUNT, BLOCK_TOKENS, D), 1.0, 6.0, ((1, 32),))
    keys = noise(key_list[1], (BLOCK_COUNT, BLOCK_TOKENS, D), 1.0, 6.0, ((1, 32),))
    values = noise(key_list[2], (BLOCK_COUNT, BLOCK_TOKENS, D), 1.0, 6.0, ((1, 32),))
    rates = jnp.clip(jnp.exp(math.log(1.0) - 2.9996462 * jax.random.uniform(key_list[3], (BLOCK_COUNT, BLOCK_TOKENS, HEADS), jnp.float32) ** shard_levels(key_list[3], (BLOCK_COUNT, BLOCK_TOKENS, HEADS), ((1, 32),), -0.2, 0.2)), 0.049804688, 1.0).astype(jnp.bfloat16)
    fast_init = noise(key_list[4], (HEADS, 3, HD, FH), HD ** -0.5, 0.25, ((0, 2), (2, 16)), jnp.float32)
    return {"queries": queries, "keys": keys, "values": values, "rates": rates, "fast_init": fast_init}


EPSILON = 1e-06
COEF_A = 3.4445
COEF_B = -4.775
COEF_C = 2.0315
LEARNING_STEP = 0.5
FULL_PRECISION = lax.Precision.HIGHEST

def silu_parts(gate_pre):
    sigmoid_value = jax.nn.sigmoid(gate_pre)
    return (gate_pre * sigmoid_value, sigmoid_value * (1.0 + gate_pre * (1.0 - sigmoid_value)))

def contract_rows(left, right):
    return lax.dot_general(left, right, (((0,), (0,)), ((), ())), preferred_element_type=jnp.float32)

def gram_of(weight_matrices):
    return jnp.einsum('qha,qhk->qak', weight_matrices, weight_matrices, precision=FULL_PRECISION)

def newton_schulz(gradients):
    gram_matrix = gram_of(gradients)
    norm_value = jnp.sqrt(jnp.trace(gram_matrix, axis1=1, axis2=2)) + EPSILON
    current_weights = gradients / norm_value[:, None, None]
    gram_matrix = gram_matrix / (norm_value * norm_value)[:, None, None]
    identity = jnp.eye(gram_matrix.shape[-1], dtype=gram_matrix.dtype)
    for sweeps in range(2):
        if sweeps > 0:
            gram_matrix = gram_of(current_weights)
        square = jnp.einsum('mfg,mgk->mfk', gram_matrix, gram_matrix, precision=FULL_PRECISION)
        polynomial_update = COEF_A * identity + COEF_B * gram_matrix + COEF_C * square
        current_weights = jnp.einsum('tid,tdp->tip', current_weights, polynomial_update, precision=FULL_PRECISION)
    return current_weights

def group_step(weights, query_rows, key_rows, value_rows, rate_rows):
    low = weights.astype(jnp.bfloat16)
    gate_pre = jnp.dot(key_rows, low[0], preferred_element_type=jnp.float32)
    up_proj = jnp.dot(key_rows, low[1], preferred_element_type=jnp.float32)
    activated_hidden, slope_value = silu_parts(gate_pre)
    hidden = (activated_hidden * up_proj).astype(jnp.bfloat16)
    out_grad = (-(rate_rows.astype(jnp.float32)[:, None] * value_rows.astype(jnp.float32))).astype(jnp.bfloat16)
    hidden_grad = jnp.dot(out_grad, low[2], preferred_element_type=jnp.float32)
    gate_grad = (hidden_grad * up_proj * slope_value).astype(jnp.bfloat16)
    up_grad = (hidden_grad * activated_hidden).astype(jnp.bfloat16)
    gradients = jnp.stack([contract_rows(key_rows, gate_grad), contract_rows(key_rows, up_grad), contract_rows(out_grad, hidden)])
    weights = weights - LEARNING_STEP * newton_schulz(gradients)
    low = weights.astype(jnp.bfloat16)
    query_gate = jnp.dot(query_rows, low[0], preferred_element_type=jnp.float32)
    query_up = jnp.dot(query_rows, low[1], preferred_element_type=jnp.float32)
    query_act, unused_slope = silu_parts(query_gate)
    query_hidden = (query_act * query_up).astype(jnp.bfloat16)
    result = lax.dot_general(query_hidden, low[2], (((1,), (1,)), ((), ())), preferred_element_type=jnp.float32)
    return (weights, result.astype(jnp.bfloat16))

def reference(queries, keys, values, rates, fast_init):

    def head_pass(head_index):
        start = (head_index * HD).astype(jnp.int32)
        query_head = lax.dynamic_slice_in_dim(queries, start, HD, 2)
        key_head = lax.dynamic_slice_in_dim(keys, start, HD, 2)
        value_head = lax.dynamic_slice_in_dim(values, start, HD, 2)
        rate_head = lax.dynamic_slice_in_dim(rates, head_index.astype(jnp.int32), 1, 2)[:, :, 0]
        weights = fast_init[head_index]
        results = []
        for group_index in range(BLOCK_COUNT):
            weights, result = group_step(weights, query_head[group_index], key_head[group_index], value_head[group_index], rate_head[group_index])
            results.append(result)
        return jnp.stack(results)
    stacked = lax.map(head_pass, jnp.arange(HEADS, dtype=jnp.int32))
    return jnp.transpose(stacked, (1, 2, 0, 3)).reshape(BLOCK_COUNT, BLOCK_TOKENS, HEADS * HD)
```

```python
import functools

import jax
import jax.numpy as jnp
from jax import lax
from jax.experimental import pallas as pl
from jax.experimental.pallas import tpu as pltpu
from jax.sharding import PartitionSpec as P

EPSILON = 1e-06
COEF_A = 3.4445
COEF_B = -4.775
COEF_C = 2.0315
LEARNING_STEP = 0.5
FULL_PRECISION = lax.Precision.HIGHEST
AXES = ("seq", "head")
GATHERED_ROWS_MAX = 2048
BF16 = jnp.bfloat16
F32 = jnp.float32


NN = (((1,), (0,)), ((), ()))
NT = (((1,), (1,)), ((), ()))
VMEM = pl.BlockSpec(memory_space=pltpu.VMEM)
SMEM = pl.BlockSpec(memory_space=pltpu.SMEM)


def dot(left, right, dims):
    return lax.dot_general(left, right, dims, preferred_element_type=F32)


def sigmoid(x):
    return 0.5 * jnp.tanh(0.5 * x) + 0.5


def pack_kd(keys, values, rates, block, head_size):
    _, rows, width = keys.shape
    heads = width // head_size

    def body(k_ref, v_ref, r_ref, o_ref):
        rate = r_ref[0].astype(F32)
        for h in range(heads):
            cols = slice(h * head_size, (h + 1) * head_size)
            o_ref[h, :rows, :] = k_ref[0, :, cols]
            o_ref[h, rows:, :] = (-(rate[:, h : h + 1] * v_ref[0, :, cols].astype(F32))).astype(BF16)

    spec = pl.BlockSpec((1, rows, width), lambda i: (block, 0, 0))
    return pl.pallas_call(
        body,
        grid=(1,),
        out_shape=jax.ShapeDtypeStruct((heads, 2 * rows, head_size), BF16),
        in_specs=[spec, spec, pl.BlockSpec((1, rows, heads), lambda i: (block, 0, 0))],
        out_specs=pl.BlockSpec((heads, 2 * rows, head_size), lambda i: (0, 0, 0)),
        name=f"pack_kd{block}",
    )(keys, values, rates)


def pack_q(queries, head_size):
    blocks, rows, width = queries.shape
    heads = width // head_size

    def body(q_ref, o_ref):
        for b in range(blocks):
            for h in range(heads):
                o_ref[h, b * rows : (b + 1) * rows, :] = q_ref[b, :, h * head_size : (h + 1) * head_size]

    return pl.pallas_call(
        body,
        out_shape=jax.ShapeDtypeStruct((heads, blocks * rows, head_size), BF16),
        in_specs=[VMEM],
        out_specs=VMEM,
        name="pack_q",
    )(queries)


def transpose_weights(pieces, scalars, low):
    shards, mats, rows, hidden = pieces[0].shape
    head_size = len(pieces) * shards * rows

    def body(s_ref, *refs):
        ins, out, acc = refs[: len(pieces)], refs[len(pieces)], refs[len(pieces) + 1]
        for p, ref in enumerate(ins):
            for q in range(shards):
                at = pl.multiple_of(s_ref[p * shards + q] * rows, rows)
                for m in range(mats):
                    acc[m, pl.ds(at, rows), :] = ref[q, m].astype(F32)
        for m in range(mats):
            out[m] = acc[m].T

    return pl.pallas_call(
        body,
        out_shape=jax.ShapeDtypeStruct((mats, hidden, head_size), F32),
        in_specs=[SMEM] + [VMEM] * len(pieces),
        out_specs=VMEM,
        scratch_shapes=[pltpu.VMEM((mats, head_size, hidden), F32)],
        name="weights_low" if low else "weights_high",
    )(scalars, *pieces)


def orthogonalized(grad):
    inv = 1.0 / (jnp.sqrt(jnp.sum(grad * grad)) + EPSILON)
    x = grad * inv
    for _ in range(2):
        xb = x.astype(BF16)
        a = dot(xb, xb, NT)
        ab = a.astype(BF16)
        poly = COEF_B * a + COEF_C * dot(ab, ab, NN)
        x = COEF_A * x + dot(poly.astype(BF16), xb, NN)
    return x


def update_step(weights, kd_parts, rows, weights_low=None):
    mats, hidden, head_size = weights.shape
    extra = [] if weights_low is None else [weights_low]

    def body(*refs):
        w_ref = refs[0]
        parts = refs[1 : 1 + len(kd_parts)]
        low_ref = refs[1 + len(kd_parts)] if extra else None
        new_ref, newb_ref = refs[-2:]
        w0, w1, w2 = (w_ref[m].astype(BF16) for m in range(3))
        gu = jnp.concatenate([w0, w1], 0)
        grad_gu = jnp.zeros((2 * hidden, head_size), F32)
        grad_d = jnp.zeros((hidden, head_size), F32)
        for ref in parts:
            step = min(8, ref.shape[0])
            for at in range(0, ref.shape[0], step):
                count = step * rows
                k = ref[at : at + step, :rows, :].reshape(count, head_size)
                d = ref[at : at + step, rows:, :].reshape(count, head_size)
                both = dot(gu, k, NT)
                g, u = both[:hidden], both[hidden:]
                dh = dot(w2, d, NT)
                sig = sigmoid(g)
                act = g * sig
                slope = sig + act * (1.0 - sig)
                hid = (act * u).astype(BF16)
                dg = (dh * u * slope).astype(BF16)
                du = (dh * act).astype(BF16)
                grad_gu += dot(jnp.concatenate([dg, du], 0), k, NN)
                grad_d += dot(hid, d, NN)
        for m, grad in enumerate((grad_gu[:hidden], grad_gu[hidden:], grad_d)):
            base = w_ref[m] if low_ref is None else w_ref[m] + low_ref[m]
            new = base - LEARNING_STEP * orthogonalized(grad)
            new_ref[m] = new
            newb_ref[m] = new.astype(BF16)

    return pl.pallas_call(
        body,
        out_shape=(
            jax.ShapeDtypeStruct(weights.shape, F32),
            jax.ShapeDtypeStruct(weights.shape, BF16),
        ),
        in_specs=[VMEM] * (1 + len(kd_parts) + len(extra)),
        out_specs=(VMEM, VMEM),
        name="update_step",
    )(weights, *kd_parts, *extra)


def apply_queries(weights_b, q_rows, block, rows, group_rows, group_cols):
    _, hidden, head_size = weights_b.shape
    count = group_rows * group_cols * rows

    def body(w_ref, q_ref, o_ref):
        q = q_ref[:, block * rows : (block + 1) * rows, :].reshape(count, head_size)
        gate = dot(q, w_ref[0], NT)
        up = dot(q, w_ref[1], NT)
        hq = (gate * sigmoid(gate) * up).astype(BF16)
        res = dot(hq, w_ref[2], NN).astype(BF16).reshape(group_rows, group_cols, rows, head_size)
        for y in range(group_rows):
            o_ref[:, y * rows : (y + 1) * rows, :] = res[y]

    return pl.pallas_call(
        body,
        out_shape=jax.ShapeDtypeStruct((group_cols, group_rows * rows, head_size), BF16),
        in_specs=[VMEM, VMEM],
        out_specs=VMEM,
        name="apply_queries",
    )(weights_b, q_rows)


def head_parallel(seq_size, head_groups, group_heads, queries, keys, values, rates, fast_init):
    inner = seq_size // group_heads
    half = inner // 2
    blocks, rows, _ = keys.shape
    mats, shard_rows = fast_init.shape[1:3]
    hidden = fast_init.shape[3]
    head_size = shard_rows * seq_size

    def flat(owner, place, group):
        return (owner * inner + place) * head_groups + group

    wide = [
        [flat(o, p, g) for g in range(head_groups) for o in range(group_heads)] for p in range(inner)
    ]

    def to_owner(x):
        return lax.all_to_all(x, AXES, 0, 0, axis_index_groups=wide, tiled=True)

    narrow = [[o * inner + p for o in range(group_heads)] for p in range(inner)]

    def over_owners(x):
        return lax.all_to_all(x, "seq", 0, 0, axis_index_groups=narrow, tiled=True)

    def swap(x, bit):
        return lax.ppermute(x, "seq", [(s, s ^ bit) for s in range(seq_size)])

    def share(x):
        across = swap(x, 2)
        both = swap(jnp.concatenate([x, across], 0), 1)
        return [jnp.concatenate([x, across], 0), both]

    kd0 = pack_kd(keys, values, rates, 0, head_size)
    w_high = fast_init.astype(BF16)
    w_low = (fast_init - w_high.astype(F32)).astype(BF16)

    high_parts = share(over_owners(w_high))
    kd0_parts = share(to_owner(kd0))
    kd1_parts = share(to_owner(pack_kd(keys, values, rates, 1, head_size)))
    q_rows = to_owner(pack_q(queries, head_size))
    low_parts = share(over_owners(w_low))

    place = lax.axis_index("seq") % inner
    order = jnp.arange(group_heads, dtype=jnp.int32) * inner
    scalars = jnp.concatenate([order + (place ^ bit) for bit in (0, 2, 1, 3)]).astype(jnp.int32)

    weights = transpose_weights(high_parts, scalars, False)
    weights_low = transpose_weights(low_parts, scalars, True)
    weights, low0 = update_step(weights, kd0_parts, rows, weights_low)
    out0 = over_owners(apply_queries(low0, q_rows, 0, rows, head_groups, group_heads))
    weights, low1 = update_step(weights, kd1_parts, rows)
    out1 = over_owners(apply_queries(low1, q_rows, 1, rows, head_groups, group_heads))

    def place_out(x):
        return jnp.transpose(x, (1, 0, 2)).reshape(x.shape[1], -1)

    return jnp.stack([place_out(out0), place_out(out1)])


def silu_parts(gate_pre):
    sigmoid_value = jax.nn.sigmoid(gate_pre)
    return (gate_pre * sigmoid_value, sigmoid_value * (1.0 + gate_pre * (1.0 - sigmoid_value)))


def local_gram(weight_matrices):
    return jnp.einsum("hmrf,hmrg->hmfg", weight_matrices, weight_matrices, precision=FULL_PRECISION)


def newton_schulz(gradients):
    gram_matrix = local_gram(gradients)
    norm_value = jnp.sqrt(jnp.trace(gram_matrix, axis1=2, axis2=3)) + EPSILON
    current_weights = gradients / norm_value[:, :, None, None]
    gram_matrix = gram_matrix / (norm_value * norm_value)[:, :, None, None]
    identity = jnp.eye(gram_matrix.shape[-1], dtype=gram_matrix.dtype)
    for sweeps in range(2):
        if sweeps > 0:
            gram_matrix = local_gram(current_weights)
        square = jnp.einsum("hmfg,hmgk->hmfk", gram_matrix, gram_matrix, precision=FULL_PRECISION)
        polynomial_update = COEF_A * identity + COEF_B * gram_matrix + COEF_C * square
        current_weights = jnp.einsum(
            "hmrf,hmfg->hmrg", current_weights, polynomial_update, precision=FULL_PRECISION
        )
    return current_weights


def token_parallel(queries, keys, values, rates, fast_init):
    weights = lax.all_gather(fast_init, "seq", axis=2, tiled=True)
    head_count = weights.shape[0]
    head_size = weights.shape[2]
    dims = functools.partial(jnp.einsum, preferred_element_type=F32)
    results = []
    for block in range(queries.shape[0]):
        query_flat, key_flat, value_flat, rate_rows = (
            lax.all_to_all(x[block], "head", split_axis=1, concat_axis=0, tiled=True)
            for x in (queries, keys, values, rates)
        )
        row_count = query_flat.shape[0]
        query_rows, key_rows, value_rows = (
            x.reshape(row_count, head_count, head_size) for x in (query_flat, key_flat, value_flat)
        )
        low = weights.astype(BF16)
        gate_pre = dims("rhd,hdf->rhf", key_rows, low[:, 0])
        up_proj = dims("rhd,hdf->rhf", key_rows, low[:, 1])
        activated_hidden, slope_value = silu_parts(gate_pre)
        hidden = (activated_hidden * up_proj).astype(BF16)
        out_grad = (-(rate_rows.astype(F32)[:, :, None] * value_rows.astype(F32))).astype(BF16)
        hidden_grad = dims("rhd,hdf->rhf", out_grad, low[:, 2])
        gate_grad = (hidden_grad * up_proj * slope_value).astype(BF16)
        up_grad = (hidden_grad * activated_hidden).astype(BF16)
        gradients = jnp.stack(
            [
                dims("rhd,rhf->hdf", key_rows, gate_grad),
                dims("rhd,rhf->hdf", key_rows, up_grad),
                dims("rhd,rhf->hdf", out_grad, hidden),
            ],
            axis=1,
        )
        weights = weights - LEARNING_STEP * newton_schulz(lax.psum(gradients, "seq"))
        low = weights.astype(BF16)
        query_act, _ = silu_parts(dims("rhd,hdf->rhf", query_rows, low[:, 0]))
        query_hidden = (query_act * dims("rhd,hdf->rhf", query_rows, low[:, 1])).astype(BF16)
        result = dims("rhf,hdf->rhd", query_hidden, low[:, 2])
        results.append(result.astype(BF16).reshape(row_count, head_count * head_size))
    return jnp.stack(results)


def solution(mesh):
    seq_size, head_groups = mesh.shape["seq"], mesh.shape["head"]

    def local(queries, keys, values, rates, fast_init):
        group_heads = fast_init.shape[0]
        inner = seq_size // group_heads if seq_size % group_heads == 0 else 0
        tokens = keys.shape[1] * seq_size * head_groups
        if inner == 4 and tokens <= GATHERED_ROWS_MAX:
            return head_parallel(seq_size, head_groups, group_heads, queries, keys, values, rates, fast_init)
        return token_parallel(queries, keys, values, rates, fast_init)

    return jax.shard_map(
        local,
        mesh=mesh,
        in_specs=(
            P(None, ("seq", "head"), None),
            P(None, ("seq", "head"), None),
            P(None, ("seq", "head"), None),
            P(None, ("seq", "head"), None),
            P("head", None, "seq", None),
        ),
        out_specs=P(None, "seq", "head"),
        check_vma=False,
    )
```

```python
import functools

import jax
import jax.numpy as jnp
from jax import lax
from jax.experimental import pallas as pl
from jax.experimental.pallas import tpu as pltpu
from jax.sharding import PartitionSpec as P


EPSILON = 1e-06
COEF_A = 3.4445
COEF_B = -4.775
COEF_C = 2.0315
LEARNING_STEP = 0.5
FULL_PRECISION = lax.Precision.HIGHEST
AXES = ("seq", "head")
GATHERED_ROWS_MAX = 2048
BF16 = jnp.bfloat16
F32 = jnp.float32


NN = (((1,), (0,)), ((), ()))
NT = (((1,), (1,)), ((), ()))
VMEM = pl.BlockSpec(memory_space=pltpu.VMEM)
SMEM = pl.BlockSpec(memory_space=pltpu.SMEM)


def dot(left, right, dims):
    return lax.dot_general(left, right, dims, preferred_element_type=F32)


def sigmoid(x):
    return 0.5 * jnp.tanh(0.5 * x) + 0.5


GRANT = pltpu.CompilerParams(vmem_limit_bytes=16 << 20)


def near(x):
    return pltpu.with_memory_space_constraint(x, pltpu.VMEM)


class Spot:
    def __init__(self, inner, group_heads):
        self.inner, self.group_heads = inner, group_heads

    def seq(self):
        return lax.axis_index("seq")

    def owner(self):
        return lax.axis_index("seq") // self.inner

    def core(self):
        return lax.axis_index("seq") % 2

    def group(self):
        return lax.axis_index("head")

    def differ(self, o):
        return o[0] + (self.core() ^ o[1]) if isinstance(o, tuple) else o

    def head(self, o, g):
        return (self.group() ^ g) * self.group_heads + (self.owner() ^ self.differ(o))


def columns(h, head_size):
    return pl.ds(pl.multiple_of(h * head_size, head_size), head_size)


def far_away(x):
    return pltpu.with_memory_space_constraint(x, pltpu.HBM)


HBM = pl.BlockSpec(memory_space=pl.ANY)


def pack_pieces(spot, keys, values, rates_t, fast_init, block, bundles, head_size):
    _, rows, width = keys.shape
    heads = width // head_size
    with_weights = fast_init is not None
    half = extra = 0
    if with_weights:
        _, mats, shard, hidden = fast_init.shape
        half = shard // 2
        extra = mats * half

    def size(g):
        return 2 * rows + (extra if g == 0 else 0)

    slots = []
    for n, peers in enumerate(bundles):
        base = 0
        for o, g in peers:
            slots.append((n, base, o, g))
            base += size(g)

    def body(*refs):
        n_in = 4 if with_weights else 3
        k_ref, v_ref, r_ref = refs[:3]
        outs = refs[n_in : n_in + len(bundles)]
        scratch = refs[n_in + len(bundles) :]
        v_buf, r_buf, sems = scratch[0], scratch[1], scratch[-1]
        copies = [pltpu.make_async_copy(r_ref.at[block], r_buf, sems.at[0])]
        for i, (n, base, o, g) in enumerate(slots):
            cols = columns(spot.head(o, g), head_size)
            copies.append(pltpu.make_async_copy(v_ref.at[block, :, cols], v_buf.at[i], sems.at[1 + 3 * i]))
            if with_weights and g == 0:
                copies.append(
                    pltpu.make_async_copy(refs[3].at[spot.owner() ^ spot.differ(o)], scratch[2].at[i], sems.at[2 + 3 * i])
                )
            copies.append(
                pltpu.make_async_copy(
                    k_ref.at[block, :, cols], outs[n].at[base : base + rows, :], sems.at[3 + 3 * i]
                )
            )
        for copy in copies:
            copy.start()
        for copy in copies:
            copy.wait()
        rate = r_buf[...].astype(F32).T
        lane = lax.broadcasted_iota(jnp.int32, rate.shape, 1)
        for i, (n, base, o, g) in enumerate(slots):
            out = outs[n]
            scale = jnp.sum(jnp.where(lane == spot.head(o, g), rate, 0.0), axis=1, keepdims=True)
            out[base + rows : base + 2 * rows, :] = (-(scale * v_buf[i].astype(F32))).astype(BF16)
            if with_weights and g == 0:
                for m in range(mats):
                    at = base + 2 * rows + m * half
                    w = scratch[2][i, m]
                    out[at : at + half, :hidden] = w[:half].astype(BF16)
                    out[at : at + half, hidden:] = w[half:].astype(BF16)

    args = [far_away(keys), far_away(values), far_away(rates_t)]
    scratch_shapes = [pltpu.VMEM((len(slots), rows, head_size), BF16), pltpu.VMEM((heads, rows), BF16)]
    if with_weights:
        args.append(far_away(fast_init))
        scratch_shapes.append(pltpu.VMEM((len(slots),) + fast_init.shape[1:], F32))
    scratch_shapes.append(pltpu.SemaphoreType.DMA((1 + 3 * len(slots),)))
    return pl.pallas_call(
        body,
        out_shape=[pltpu.VMEM((sum(size(g) for _, g in peers), head_size), BF16) for peers in bundles],
        in_specs=[HBM] * len(args),
        out_specs=[VMEM for _ in bundles],
        scratch_shapes=scratch_shapes,
        compiler_params=GRANT,
    )(*args)


def pack_queries(spot, queries, bundles, head_size):
    blocks, rows, _ = queries.shape

    def body(q_ref, *refs):
        outs, sem = refs[:-1], refs[-1]
        copies = []
        for peers, out in zip(bundles, outs):
            for i, (o, g) in enumerate(peers):
                cols = columns(spot.head(o, g), head_size)
                for b in range(blocks):
                    at = (i * blocks + b) * rows
                    copies.append(
                        pltpu.make_async_copy(q_ref.at[b, :, cols], out.at[at : at + rows, :], sem.at[len(copies)])
                    )
        for copy in copies:
            copy.start()
        for copy in copies:
            copy.wait()

    pieces = sum(len(peers) for peers in bundles)
    return pl.pallas_call(
        body,
        out_shape=[pltpu.VMEM((len(peers) * blocks * rows, head_size), BF16) for peers in bundles],
        in_specs=[HBM],
        out_specs=[VMEM for _ in bundles],
        scratch_shapes=[pltpu.SemaphoreType.DMA((pieces * blocks,))],
        name="pack_q",
        compiler_params=GRANT,
    )(far_away(queries))


def join(*groups):
    arrays = []
    for group in groups:
        for x, _, _ in group:
            if not any(x is y for y in arrays):
                arrays.append(x)

    def body(*refs):
        outs = refs[len(arrays) :]
        for group, out in zip(groups, outs):
            to = 0
            for x, at, count in group:
                ref = refs[[x is y for y in arrays].index(True)]
                out[to : to + count, :] = ref[at : at + count, :]
                to += count

    width = arrays[0].shape[1]
    return pl.pallas_call(
        body,
        out_shape=[pltpu.VMEM((sum(c for _, _, c in group), width), BF16) for group in groups],
        in_specs=[VMEM] * len(arrays),
        out_specs=[VMEM] * len(groups),
        compiler_params=GRANT,
    )(*(near(x) for x in arrays))


def orthogonalized(grads):
    xs = [g * (1.0 / (jnp.sqrt(jnp.sum(g * g)) + EPSILON)) for g in grads]
    for _ in range(2):
        xbs = [x.astype(BF16) for x in xs]
        grams = [dot(x, x, NT) for x in xbs]
        lows = [a.astype(BF16) for a in grams]
        polys = [(COEF_B * a + COEF_C * dot(b, b, NN)).astype(BF16) for a, b in zip(grams, lows)]
        xs = [COEF_A * x + dot(p, xb, NN) for x, p, xb in zip(xs, polys, xbs)]
    return xs


def gradients(w0, w1, w2, refs, segments, rows, out_ref, before=None):
    hidden, _ = w0.shape
    gu = jnp.concatenate([w0, w1], 0)
    most = 8
    for at in range(0, len(segments), most):
        chunk = segments[at : at + most]
        k = jnp.concatenate([refs[i][to : to + rows, :] for i, to in chunk], 0)
        d = jnp.concatenate([refs[i][to + rows : to + 2 * rows, :] for i, to in chunk], 0)
        both = dot(gu, k, NT)
        g, u = both[:hidden], both[hidden:]
        dh = dot(w2, d, NT)
        sig = sigmoid(g)
        act = g * sig
        slope = sig + act * (1.0 - sig)
        hid = (act * u).astype(BF16)
        dg = (dh * u * slope).astype(BF16)
        du = (dh * act).astype(BF16)
        for m, part in enumerate((dot(dg, k, NN), dot(du, k, NN), dot(hid, d, NN))):
            if at:
                part = out_ref[m] + part
            elif before is not None:
                part = before[m] + part
            out_ref[m] = part


def first_gradients(spot, parts, segments, shards, rows, mats, hidden):
    head_size = parts[0].shape[1]
    half = head_size // len(shards) // 2

    def body(*refs):
        ins = refs[: len(parts)]
        old_ref, grad_ref, acc = refs[-3:]
        for i, at, differs, core in shards:
            source = spot.seq() ^ differs
            if core is not None:
                source = source ^ ((spot.core() ^ core) * spot.inner)
            to = source * (2 * half)
            for m in range(mats):
                piece = ins[i][at + m * half : at + (m + 1) * half, :].astype(F32)
                acc[m, pl.ds(pl.multiple_of(to, half), half), :] = piece[:, :hidden]
                acc[m, pl.ds(pl.multiple_of(to + half, half), half), :] = piece[:, hidden:]
        old = [acc[m].T for m in range(mats)]
        for m in range(mats):
            old_ref[m] = old[m]
        gradients(*(w.astype(BF16) for w in old), ins, segments, rows, grad_ref)

    shape = (mats, hidden, head_size)
    return pl.pallas_call(
        body,
        out_shape=(pltpu.VMEM(shape, F32), pltpu.VMEM(shape, F32)),
        in_specs=[VMEM] * len(parts),
        out_specs=(VMEM, VMEM),
        scratch_shapes=[pltpu.VMEM((mats, head_size, hidden), F32)],
        name="grads0",
        compiler_params=GRANT,
    )(*(near(p) for p in parts))


def early_gradients(weights_b, parts, segments, rows):
    def body(*refs):
        wb_ref = refs[0]
        gradients(wb_ref[0], wb_ref[1], wb_ref[2], refs[1 : 1 + len(parts)], segments, rows, refs[-1])

    return pl.pallas_call(
        body,
        out_shape=pltpu.VMEM(weights_b.shape, F32),
        in_specs=[VMEM] * (1 + len(parts)),
        out_specs=VMEM,
        name="grads1",
        compiler_params=GRANT,
    )(near(weights_b), *(near(p) for p in parts))


def step(weights, early, parts, segments, rows, last):
    def body(*refs):
        w_ref, early_ref = refs[:2]
        outs, grad_ref = refs[2 + len(parts) : -1], refs[-1]
        mats = range(w_ref.shape[0])
        low = [w_ref[m].astype(BF16) for m in mats]
        gradients(*low, refs[2 : 2 + len(parts)], segments, rows, grad_ref, early_ref)
        for m, x in zip(mats, orthogonalized([grad_ref[m] for m in mats])):
            new = w_ref[m] - LEARNING_STEP * x
            outs[0][m] = new.astype(BF16)
            if not last:
                outs[1][m] = new

    kinds = (BF16,) if last else (BF16, F32)
    return pl.pallas_call(
        body,
        out_shape=[pltpu.VMEM(weights.shape, kind) for kind in kinds],
        in_specs=[VMEM] * (2 + len(parts)),
        out_specs=[VMEM] * len(kinds),
        scratch_shapes=[pltpu.VMEM(weights.shape, F32)],
        compiler_params=GRANT,
    )(near(weights), near(early), *(near(p) for p in parts))


def apply_queries(spot, low, parts, segments, block, rows, pairs, head_groups):
    _, _, head_size = low.shape

    def body(w_ref, *refs):
        qs, outs = refs[: len(parts)], refs[len(parts) :]
        q = jnp.concatenate([qs[s[0]][s[1] + block * rows : s[1] + (block + 1) * rows, :] for s in segments], 0)
        gate = dot(q, w_ref[0], NT)
        up = dot(q, w_ref[1], NT)
        hq = (gate * sigmoid(gate) * up).astype(BF16)
        res = dot(hq, w_ref[2], NN).astype(BF16)
        for n, (_, _, pair, home, g) in enumerate(segments):
            to = pl.multiple_of((home * head_groups + (spot.group() ^ g)) * rows, rows)
            outs[pair][pl.ds(to, rows), :] = res[n * rows : (n + 1) * rows]

    return pl.pallas_call(
        body,
        out_shape=[pltpu.VMEM((2 * head_groups * rows, head_size), BF16) for _ in range(pairs)],
        in_specs=[VMEM] * (1 + len(parts)),
        out_specs=[VMEM] * pairs,
        compiler_params=GRANT,
    )(near(low), *(near(p) for p in parts))


def place_outputs(spot, got, other, tokens, group_heads):
    blocks, pairs = len(got), len(got[0])
    head_size = other[0].shape[1]

    def body(*refs):
        out, sems = refs[-2:]
        copies = []
        for b in range(blocks):
            mate = refs[blocks * pairs + b]
            for k in range(pairs):
                for core, source in ((0, refs[b * pairs + k].at[:tokens]), (1, mate.at[k * tokens : (k + 1) * tokens])):
                    to = out.at[b, :, columns(spot.owner() ^ spot.differ((2 * k, core)), head_size)]
                    copies.append(pltpu.make_async_copy(source, to, sems.at[len(copies)]))
        for copy in copies:
            copy.start()
        for copy in copies:
            copy.wait()

    return pl.pallas_call(
        body,
        out_shape=jax.ShapeDtypeStruct((blocks, tokens, group_heads * head_size), BF16),
        in_specs=[VMEM] * (blocks * (pairs + 1)),
        out_specs=HBM,
        scratch_shapes=[pltpu.SemaphoreType.DMA((2 * blocks * pairs,))],
        name="place",
        compiler_params=GRANT,
    )(*(near(x) for x in [*[x for xs in got for x in xs], *other]))


class Network:
    def __init__(self, seq_size, head_groups, inner):
        self.seq_size, self.head_groups, self.inner = seq_size, head_groups, inner

    def send(self, x, o=0, i=0, g=0, by_core=False):
        def move(s):
            return (o + (s % 2 if by_core else 0)) * self.inner + i

        pairs = [
            (s * self.head_groups + y, (s ^ move(s)) * self.head_groups + (y ^ g))
            for s in range(self.seq_size)
            for y in range(self.head_groups)
        ]
        return lax.ppermute(x, AXES, pairs)


def head_parallel(seq_size, head_groups, group_heads, queries, keys, values, rates, fast_init):
    inner = seq_size // group_heads
    net, spot = Network(seq_size, head_groups, inner), Spot(inner, group_heads)
    rows = keys.shape[1]
    blocks = queries.shape[0]
    mats, shard_rows, hidden = fast_init.shape[1:]
    head_size = shard_rows * seq_size
    weight_rows = mats * (shard_rows // 2)
    owners = range(group_heads)
    rates_t = jnp.transpose(rates, (0, 2, 1))

    def whole(*xs):
        return [(x, 0, x.shape[0]) for x in xs]

    far = list(owners)[2:]
    evens = list(owners)[::2]
    groups = range(head_groups)
    me, mate = [(e, 0) for e in evens], [(e, 1) for e in evens]
    all_kept = [(e, g) for e in me for g in groups]
    all_given = [(e, g) for e in mate for g in groups]
    kept = [p for p in all_kept if p[1] or not p[0][0]]
    given = [p for p in all_given if p[1] or not p[0][0]]
    packed = pack_pieces(
        spot, keys, values, rates_t, fast_init, 0,
        [[(o, 0)] for o in far] + [[p] for p in kept] + [given], head_size,
    )
    straight = [net.send(x, o=o) for o, x in zip(far, packed)]

    def paired(mine, swapped, base):
        lists, at = [], base
        for x in mine:
            lists.append([(x, 0, x.shape[0]), (swapped, at, x.shape[0])])
            at += x.shape[0]
        return lists

    swapped = net.send(packed[-1], i=1)
    loads0 = dict(zip(kept, join(*paired(packed[len(far) : -1], swapped, 0))))

    packed1 = pack_pieces(spot, keys, values, rates_t, None, 1, [[p] for p in all_kept] + [all_given], head_size)
    packed_q = pack_queries(spot, queries, [[p] for p in all_kept] + [all_given], head_size)
    swapped = net.send(join(whole(packed1[-1], packed_q[-1]))[0], i=1)
    lists1 = paired(packed1[:-1], swapped, 0)
    lists_q = paired(packed_q[:-1], swapped, packed1[-1].shape[0])
    joined, far_lists = [], []
    for p, x, y in zip(all_kept, lists1, lists_q):
        if p[0][0]:
            far_lists += [x, y]
        else:
            joined.append(x + y)
    loads = join(*joined, *far_lists)

    def to_peer(x, e, g, i=0):
        return net.send(x, o=e, i=i, g=g, by_core=True)

    close0 = [to_peer(loads0[(me[0], g)], 0, g) for g in groups]
    close = [to_peer(x, 0, g) for g, x in zip(groups, loads)]
    beside = [to_peer(loads0[(me[0], g)], 0, g, i=2) for g in groups]
    distant0 = [to_peer(loads0[p], p[0][0], p[1]) for p in kept if p[0][0]]
    distant1, distant_q = [], []
    for n, (e, g) in enumerate(p for p in all_kept if p[0][0]):
        distant1.append(to_peer(loads[head_groups + 2 * n], e[0], g))
        distant_q.append(to_peer(loads[head_groups + 2 * n + 1], e[0], g))

    per, per_q = 2 * rows, blocks * rows
    distant0 = distant0[0] if len(distant0) == 1 else join(whole(*distant0))[0]
    direct = join(whole(*straight))[0]
    both_cores = (0, 1)
    parts0, segments0, shards0 = [], [], []
    for mine, layout in (
        (None, [(0, g, c) for g in groups for c in both_cores]),
        (direct, [(o, 0, None) for o in far]),
        (distant0, [(e, g, c) for e in evens[1:] for g in groups[1:] for c in both_cores]),
    ):
        if mine is None:
            pair = join(whole(*close0, *beside))[0]
        else:
            pair = join(whole(mine, net.send(mine, i=2)))[0]
        for holder, array in ((0, pair), (1, net.send(pair, i=1))):
            at = 0
            for x in (0, 2):
                for o, g, c in layout:
                    segments0.append((len(parts0), at))
                    at += per
                    if g == 0:
                        core = holder if c is None else holder ^ c
                        shards0.append((len(parts0), at, o * inner + x + core, None if c is None else holder))
                        at += weight_rows
            parts0.append(array)

    parts1 = []
    for some in ([(x, 0, 2 * per) for x in close], whole(*distant1)):
        mine = join(some)[0]
        across = net.send(mine, i=2)
        parts1 += [mine, across, net.send(mine, i=1), net.send(across, i=1)]
    segments1 = [(n, at) for n, part in enumerate(parts1) for at in range(0, part.shape[0], per)]

    q_parts = close + distant_q
    segments_q = []
    for n, (e, g) in enumerate(all_kept):
        for home in both_cores:
            at = 2 * per if n < head_groups else 0
            segments_q.append((n, at + home * per_q, e[0] // 2, home, g))

    half = head_groups * rows

    def outputs(block, low):
        mine = apply_queries(spot, low, q_parts, segments_q, block, rows, len(evens), head_groups)
        return [net.send(x, o=e, by_core=True) for e, x in zip(evens, mine)]

    def cut(parts, segments, early):
        return (
            (parts[:early], [x for x in segments if x[0] < early]),
            (parts[early:], [(n - early, at) for n, at in segments if n >= early]),
        )

    (parts_e, segments_e), (parts_l, segments_l) = cut(parts0, segments0, 4)
    weights, grads = first_gradients(spot, parts_e, segments_e, shards0, rows, mats, hidden)
    low, weights = step(weights, grads, parts_l, segments_l, rows, False)
    got = [outputs(0, low)]
    (parts_e, segments_e), (parts_l, segments_l) = cut(parts1, segments1, len(parts1) // 2)
    grads = early_gradients(low, parts_e, segments_e, rows)
    low = step(weights, grads, parts_l, segments_l, rows, True)[0]
    got.append(outputs(1, low))
    other = [net.send(join([(x, half, half) for x in xs])[0], i=1) for xs in got]
    return place_outputs(spot, got, other, half, group_heads)


def silu_parts(gate_pre):
    sigmoid_value = jax.nn.sigmoid(gate_pre)
    return (gate_pre * sigmoid_value, sigmoid_value * (1.0 + gate_pre * (1.0 - sigmoid_value)))


def local_gram(weight_matrices):
    return jnp.einsum("hmrf,hmrg->hmfg", weight_matrices, weight_matrices, precision=FULL_PRECISION)


def newton_schulz(gradients):
    gram_matrix = local_gram(gradients)
    norm_value = jnp.sqrt(jnp.trace(gram_matrix, axis1=2, axis2=3)) + EPSILON
    current_weights = gradients / norm_value[:, :, None, None]
    gram_matrix = gram_matrix / (norm_value * norm_value)[:, :, None, None]
    identity = jnp.eye(gram_matrix.shape[-1], dtype=gram_matrix.dtype)
    for sweeps in range(2):
        if sweeps > 0:
            gram_matrix = local_gram(current_weights)
        square = jnp.einsum("hmfg,hmgk->hmfk", gram_matrix, gram_matrix, precision=FULL_PRECISION)
        polynomial_update = COEF_A * identity + COEF_B * gram_matrix + COEF_C * square
        current_weights = jnp.einsum(
            "hmrf,hmfg->hmrg", current_weights, polynomial_update, precision=FULL_PRECISION
        )
    return current_weights


def token_parallel(queries, keys, values, rates, fast_init):
    weights = lax.all_gather(fast_init, "seq", axis=2, tiled=True)
    head_count = weights.shape[0]
    head_size = weights.shape[2]
    dims = functools.partial(jnp.einsum, preferred_element_type=F32)
    results = []
    for block in range(queries.shape[0]):
        query_flat, key_flat, value_flat, rate_rows = (
            lax.all_to_all(x[block], "head", split_axis=1, concat_axis=0, tiled=True)
            for x in (queries, keys, values, rates)
        )
        row_count = query_flat.shape[0]
        query_rows, key_rows, value_rows = (
            x.reshape(row_count, head_count, head_size) for x in (query_flat, key_flat, value_flat)
        )
        low = weights.astype(BF16)
        gate_pre = dims("rhd,hdf->rhf", key_rows, low[:, 0])
        up_proj = dims("rhd,hdf->rhf", key_rows, low[:, 1])
        activated_hidden, slope_value = silu_parts(gate_pre)
        hidden = (activated_hidden * up_proj).astype(BF16)
        out_grad = (-(rate_rows.astype(F32)[:, :, None] * value_rows.astype(F32))).astype(BF16)
        hidden_grad = dims("rhd,hdf->rhf", out_grad, low[:, 2])
        gate_grad = (hidden_grad * up_proj * slope_value).astype(BF16)
        up_grad = (hidden_grad * activated_hidden).astype(BF16)
        gradients = jnp.stack(
            [
                dims("rhd,rhf->hdf", key_rows, gate_grad),
                dims("rhd,rhf->hdf", key_rows, up_grad),
                dims("rhd,rhf->hdf", out_grad, hidden),
            ],
            axis=1,
        )
        weights = weights - LEARNING_STEP * newton_schulz(lax.psum(gradients, "seq"))
        low = weights.astype(BF16)
        query_act, _ = silu_parts(dims("rhd,hdf->rhf", query_rows, low[:, 0]))
        query_hidden = (query_act * dims("rhd,hdf->rhf", query_rows, low[:, 1])).astype(BF16)
        result = dims("rhf,hdf->rhd", query_hidden, low[:, 2])
        results.append(result.astype(BF16).reshape(row_count, head_count * head_size))
    return jnp.stack(results)


def solution(mesh):
    seq_size, head_groups = mesh.shape["seq"], mesh.shape["head"]

    def local(queries, keys, values, rates, fast_init):
        group_heads = fast_init.shape[0]
        inner = seq_size // group_heads if seq_size % group_heads == 0 else 0
        tokens = keys.shape[1] * seq_size * head_groups
        if inner == 4 and group_heads >= 4 and tokens <= GATHERED_ROWS_MAX:
            return head_parallel(seq_size, head_groups, group_heads, queries, keys, values, rates, fast_init)
        return token_parallel(queries, keys, values, rates, fast_init)

    return jax.shard_map(
        local,
        mesh=mesh,
        in_specs=(
            P(None, ("seq", "head"), None),
            P(None, ("seq", "head"), None),
            P(None, ("seq", "head"), None),
            P(None, ("seq", "head"), None),
            P("head", None, "seq", None),
        ),
        out_specs=P(None, "seq", "head"),
        check_vma=False,
    )
```
